768 devices in a mesh: adapter: 24 (over z, core), tensor: 32 (over y, x).
Axes of the slice: x: 4, y: 8, z: 12, core: 2. Of those that a mesh axis runs over, the one named last changes fastest.
Arguments:
- rollout_activations: bfloat16 [6144, 8192], P('adapter'), may hold values from -6 to 6
- projection_weight: bfloat16 [8192, 8192], P(None, 'tensor'), may hold values from -0.0625 to 0.0625
- adapter_down_panels: bfloat16 [384, 64, 8192], P('adapter', None, 'tensor'), may hold values from -0.0625 to 0.0625
- adapter_up_panels: bfloat16 [384, 64, 8192], P('adapter', None, 'tensor'), may hold values from -0.75 to 0.75
- output_gradient: bfloat16 [6144, 8192], P('adapter', 'tensor'), may hold values from -1.5 to 1.5
- segment_adapter: int32 [48], replicated, may hold values from 0 to 383, as said below
Outputs:
- projection_output: bfloat16 [6144, 8192], P('adapter', 'tensor')
- gradient_of_input: bfloat16 [6144, 8192], P('adapter', 'tensor')
- down_grad: bfloat16 [384, 64, 8192], P('adapter', None, 'tensor')
- up_grad: bfloat16 [384, 64, 8192], P('adapter', None, 'tensor')
The draws below stay inside these ranges and needn't reach their ends.
Inputs may be any that keep to these rules, and one draw needn't show every extreme that they name: `segment_adapter`: among the adapters of one owner, o * 16 to (o + 1) * 16 - 1, at most 2 distinct ones are named; some owner has exactly 2 named, and some segment names adapter 384 - 1.
All inputs are finite; a program needn't handle non-finite values.
Results may differ from the reference program's by a relative error of at most 0.02.
Values may be sent and summed in bfloat16 or wider, within the bound.
A program may use at most 64 MiB of HBM per device.

```python
import jax
import jax.numpy as jnp
from jax import lax

MODEL_WIDTH = 8192
ADAPTER_RANK = 64
SEG_ROWS = 128
SEG_GRP = 2
ADP_OWN = 16
ACTIVE = 2
SEGS = 48
ROW_TOTAL = 6144
ADAPTER_TOTAL = 384
N_TENSOR = 32


def pick_locals(sub_key):
    return jax.random.permutation(sub_key, ADP_OWN)[:ACTIVE].astype(jnp.int32)


def draw_segment_adapter(key, part):
    owner_count = ADAPTER_TOTAL // ADP_OWN
    key_order, key_first, key_second, key_cand, key_choice, key_shuffle = jax.random.split(key, 6)
    key_last = jax.random.fold_in(key, 977)
    owner_order = jax.random.permutation(key_order, owner_count)
    first_draw = jax.random.randint(key_first, (SEGS,), 0, owner_count)
    second_draw = jax.random.randint(key_second, (SEGS,), 0, owner_count)
    owner_of = owner_order[jnp.minimum(first_draw, second_draw)]
    candidates = jax.vmap(pick_locals)(jax.random.split(key_cand, owner_count))
    last_rest = jax.random.permutation(key_last, ADP_OWN - 1)[:ACTIVE - 1].astype(jnp.int32)
    last_row = jnp.concatenate([jnp.full((1,), ADP_OWN - 1, jnp.int32), last_rest])
    candidates = candidates.at[owner_count - 1].set(last_row)
    cand_index = jax.random.randint(key_choice, (SEGS,), 0, ACTIVE)
    position = jnp.arange(SEGS, dtype=jnp.int32)
    forced = position < ACTIVE
    owner_of = jnp.where(forced, owner_order[0], owner_of)
    cand_index = jnp.where(forced, position, cand_index)
    top_slot = position == ACTIVE
    owner_of = jnp.where(top_slot, owner_count - 1, owner_of)
    cand_index = jnp.where(top_slot, 0, cand_index)
    local_pick = candidates[owner_of, cand_index]
    adapter_ids = owner_of * ADP_OWN + local_pick
    shuffle = jax.random.permutation(key_shuffle, SEGS)
    return adapter_ids[shuffle].astype(jnp.int32)


def steps_of(own_key, extent, cuts, low, high):
    factor_of = 1.0
    for dim, parts in cuts:
        heights = jax.random.uniform(jax.random.fold_in(jax.random.fold_in(own_key, 6), dim), (parts,), jnp.float32, low / len(cuts), high / len(cuts))
        factor_of = factor_of * jnp.repeat(jnp.exp(heights), extent[dim] // parts).reshape((-1,) + (1,) * (len(extent) - 1 - dim))
    return factor_of


def normal_values(rng, dims, scale, limit, pieces=(), kind=jnp.bfloat16):
    values = scale * jax.random.normal(rng, dims, jnp.float32)
    if pieces:
        values = values * steps_of(rng, dims, pieces, -0.22, 0.18)
    return jnp.clip(values, -limit, limit).astype(kind)


def setup_inputs(seed: int = 0) -> dict:
    streams_of = jax.random.split(jax.random.key(seed), 7)
    rollout_activations = normal_values(streams_of[0], (ROW_TOTAL, MODEL_WIDTH), 1.0, 6.0, ((0, 24),))
    projection_weight = normal_values(streams_of[1], (MODEL_WIDTH, MODEL_WIDTH), MODEL_WIDTH ** -0.5, 0.0625, ((1, 32),))
    adapter_down_panels = normal_values(streams_of[2], (ADAPTER_TOTAL, ADAPTER_RANK, MODEL_WIDTH), MODEL_WIDTH ** -0.5, 0.0625, ((0, 24), (2, 32)))
    adapter_up_panels = normal_values(streams_of[3], (ADAPTER_TOTAL, ADAPTER_RANK, MODEL_WIDTH), ADAPTER_RANK ** -0.5, 0.75, ((0, 24), (2, 32)))
    output_gradient = normal_values(streams_of[4], (ROW_TOTAL, MODEL_WIDTH), 0.25, 1.5, ((0, 24), (1, 32)))
    segment_adapter = draw_segment_adapter(jax.random.fold_in(streams_of[6], 71), 0)
    return dict(rollout_activations=rollout_activations, projection_weight=projection_weight, adapter_down_panels=adapter_down_panels, adapter_up_panels=adapter_up_panels, output_gradient=output_gradient, segment_adapter=segment_adapter)


adapter_scale = 0.5


def thin_rank_value(value):
    return lax.optimization_barrier(value.astype(jnp.bfloat16)).astype(jnp.float32)


def reference(rollout_activations, projection_weight, adapter_down_panels, adapter_up_panels, output_gradient, segment_adapter):
    col_width = MODEL_WIDTH // N_TENSOR
    seg_inputs = rollout_activations.reshape(SEGS, SEG_ROWS, MODEL_WIDTH).astype(jnp.float32)
    segment_gradients = output_gradient.reshape(SEGS, SEG_ROWS, MODEL_WIDTH).astype(jnp.float32)
    selected_down_panels = adapter_down_panels[segment_adapter].astype(jnp.float32)
    selected_up_panels = adapter_up_panels[segment_adapter].astype(jnp.float32)
    low_rank = jnp.einsum("srd,skd->srk", seg_inputs, selected_down_panels)
    lowrank_halfprec = thin_rank_value(low_rank)
    frozen_output = jnp.dot(rollout_activations, projection_weight, preferred_element_type=jnp.float32)
    adapter_output = jnp.einsum("ghi,gip->ghp", lowrank_halfprec, selected_up_panels).reshape(ROW_TOTAL, MODEL_WIDTH)
    projection_output = (frozen_output + adapter_scale * adapter_output).astype(jnp.bfloat16)
    backward_rank_terms = jnp.einsum("srd,skd->srk", segment_gradients, selected_up_panels)
    backward_halfprec = thin_rank_value(adapter_scale * backward_rank_terms)

    def add_block(running, block_index):
        grad_block = lax.dynamic_slice_in_dim(output_gradient, block_index * col_width, col_width, 1)
        weight_block = lax.dynamic_slice_in_dim(projection_weight, block_index * col_width, col_width, 1)
        block_term = lax.dot_general(grad_block, weight_block, (((1,), (1,)), ((), ())), preferred_element_type=jnp.float32)
        return running + thin_rank_value(block_term), None

    frozen_backward, unused = lax.scan(add_block, jnp.zeros((ROW_TOTAL, MODEL_WIDTH), jnp.float32), jnp.arange(N_TENSOR, dtype=jnp.int32))
    adapter_backward = jnp.einsum("ghi,gip->ghp", backward_halfprec, selected_down_panels).reshape(ROW_TOTAL, MODEL_WIDTH)
    gradient_of_input = (frozen_backward + adapter_backward).astype(jnp.bfloat16)

    down_terms = jnp.einsum("iap,iaj->ipj", backward_halfprec, seg_inputs)
    upward_terms = adapter_scale * jnp.einsum("iap,iaj->ipj", lowrank_halfprec, segment_gradients)
    seg_pos = jnp.arange(SEGS, dtype=jnp.int32)
    group_of = seg_pos // SEG_GRP
    same_group = (segment_adapter[:, None] == segment_adapter[None, :]) & (group_of[:, None] == group_of[None, :])
    earlier = seg_pos[:, None] > seg_pos[None, :]
    leading = jnp.logical_not(jnp.any(same_group & earlier, axis=1)).astype(jnp.float32)
    same_weight = same_group.astype(jnp.float32)
    down_lead = thin_rank_value(jnp.einsum("st,tkd->skd", same_weight, down_terms)) * leading[:, None, None]
    up_lead = thin_rank_value(jnp.einsum("st,tkd->skd", same_weight, upward_terms)) * leading[:, None, None]
    down_grad = jax.ops.segment_sum(down_lead, segment_adapter, num_segments=ADAPTER_TOTAL).astype(jnp.bfloat16)
    up_grad = jax.ops.segment_sum(up_lead, segment_adapter, num_segments=ADAPTER_TOTAL).astype(jnp.bfloat16)
    return (projection_output, gradient_of_input, down_grad, up_grad)
```

```python
import functools

import jax
import jax.numpy as jnp
from jax import lax
from jax.experimental import pallas as pl
from jax.experimental.pallas import tpu as pltpu
from jax.sharding import PartitionSpec as P

SEG_ROWS = 128
ADP_OWN = 16
ACTIVE = 2
RANK = 64
COLS = 256
X_CHIPS = 4
MESH = pl.DeviceIdType.MESH
F32 = jnp.float32
BF16 = jnp.bfloat16

adapter_scale = 0.5


def dot(a, b, ca, cb):
    return lax.dot_general(a, b, (((ca,), (cb,)), ((), ())), preferred_element_type=F32)


def chains_of(n):
    half = n // 2
    chains, base = [], 0
    for sign, part, length in ((1, 0, half), (-1, 1, half), (1, 1, half - 1), (-1, 0, half - 1)):
        if length:
            chains.append((sign, part, length, base))
            base += length
    return chains, base


class RingSum:
    def __init__(self, n, pos, device_of, src, land, send_sem, recv_sem):
        self.n, self.pos, self.device_of = n, pos, device_of
        self.src, self.land, self.send_sem, self.recv_sem = src, land, send_sem, recv_sem
        self.chains, _ = chains_of(n)
        self.steps = n // 2

    def at(self, offset):
        return lax.rem(self.pos + offset + self.n, self.n)

    def copy(self, src, slot, sign):
        return pltpu.make_async_remote_copy(
            src_ref=src,
            dst_ref=self.land.at[slot],
            send_sem=self.send_sem,
            recv_sem=self.recv_sem.at[slot],
            device_id={"tensor": self.device_of(self.at(sign))},
            device_id_type=MESH,
        )

    def start(self):
        for sign, part, length, base in self.chains:
            self.copy(self.src.at[self.at(sign * length), part], base, sign).start()

    def step(self, s):
        for sign, part, length, base in self.chains:
            if s >= length - 1:
                continue
            slot = base + s
            self.copy(self.land.at[slot], slot, sign).wait_recv()
            place = self.at(sign * (length - s - 1))
            self.add(slot, place, part)
            self.copy(self.land.at[slot], slot + 1, sign).start()

    def add(self, slot, place, part):
        if len(self.land.shape) == 3:
            total = self.land[slot].astype(F32) + self.src[place, part].astype(F32)
            self.land[slot] = total.astype(BF16)
            return

        def body(j, carry):
            total = self.land[slot, j].astype(F32) + self.src[place, part, j].astype(F32)
            self.land[slot, j] = total.astype(BF16)
            return carry

        lax.fori_loop(0, self.land.shape[1], body, 0)

    def finish(self):
        for sign, part, length, base in self.chains:
            slot = base + length - 1
            self.copy(self.land.at[slot], slot, sign).wait_recv()

    def lasts(self, part):
        return [base + length - 1 for _, p, length, base in self.chains if p == part]

    def total(self, part, *index):
        value = self.src[(self.pos, part) + index].astype(F32)
        for slot in self.lasts(part):
            value = value + self.land[(slot,) + index].astype(F32)
        return value

    def drain(self):
        whole = self.src.at[pl.ds(0, self.n - 1)]
        pltpu.make_async_remote_copy(
            src_ref=whole,
            dst_ref=whole,
            send_sem=self.send_sem,
            recv_sem=self.recv_sem.at[0],
            device_id={"tensor": self.device_of(self.at(1))},
            device_id_type=MESH,
        ).wait_send()


class RingGather:
    def __init__(self, n, z, core, own, out, send_sem, recv_sem, pair_sem, own_sem):
        self.n, self.z, self.core = n, z, core
        self.own, self.out = own, out
        self.send_sem, self.recv_sem, self.pair_sem, self.own_sem = send_sem, recv_sem, pair_sem, own_sem
        self.steps = n // 2

    def has(self, d, k, ch):
        return k < self.steps - 1 or (k == self.steps - 1 and d == ch)

    def rows(self, z, core, ch):
        return self.out.at[pl.ds((z * 2 + core) * 4 + ch * 2, 2)]

    def ring(self, src, dst, d, k, ch):
        sign = 1 - 2 * d
        z_to = lax.rem(self.z + sign + self.n, self.n)
        return pltpu.make_async_remote_copy(
            src_ref=src,
            dst_ref=dst,
            send_sem=self.send_sem,
            recv_sem=self.recv_sem.at[d, k, ch],
            device_id={"adapter": z_to * 2 + self.core},
            device_id_type=MESH,
        )

    def pair(self, src, dst):
        return pltpu.make_async_remote_copy(
            src_ref=src,
            dst_ref=dst,
            send_sem=self.send_sem,
            recv_sem=self.pair_sem,
            device_id={"adapter": self.z * 2 + 1 - self.core},
            device_id_type=MESH,
        )

    def own_copy(self):
        return pltpu.make_async_copy(
            self.own, self.out.at[pl.ds((self.z * 2 + self.core) * 4, 4)], self.own_sem
        )

    def start(self):
        for ch in range(2):
            src, dst = self.own.at[pl.ds(ch * 2, 2)], self.rows(self.z, self.core, ch)
            for d in range(2):
                if self.has(d, 0, ch):
                    self.ring(src, dst, d, 0, ch).start()
        for ch in range(2):
            src, dst = self.own.at[pl.ds(ch * 2, 2)], self.rows(self.z, self.core, ch)
            self.pair(src, dst).start()
        self.own_copy().start()

    def step(self, k):
        for ch in range(2):
            for d in range(2):
                if not self.has(d, k, ch):
                    continue
                sign = 1 - 2 * d
                z_from = lax.rem(self.z - sign * (k + 1) + 2 * self.n, self.n)
                block = self.rows(z_from, self.core, ch)
                self.ring(block, block, d, k, ch).wait_recv()
                if self.has(d, k + 1, ch):
                    self.ring(block, block, d, k + 1, ch).start()
                self.pair(block, block).start()

    def finish(self):
        self.own_copy().wait()
        half = self.out.at[pl.ds(0, self.n * 4)]
        self.pair(half, half).wait_recv()

    def drain(self):
        sent = self.out.at[pl.ds(0, (4 * self.n - 2) * 2)]
        self.pair(sent, sent).wait_send()


def step_kernel(
    owners, tensors,
    idx, mask, x_hbm, w_hbm, down_ref, up_ref, g_ref,
    po_ref, gi_ref, dg_ref, ug_ref,
    xv, wv, acc, pk, ga, gk, gb, f1, f2, r1, r2, s1, s2, q1, q2, part, inbox, mine, total,
    in_sem, own_sem, gs_a, gr_a, gp_a, gs_b, gr_b, gp_b,
    s_r1, v_r1, s_r2, v_r2, s_q1, v_q1, s_q2, v_q2, ar_send, ar_recv,
):
    nz, nx = owners // 2, X_CHIPS
    ny = tensors // nx
    hx, hy = nx // 2, ny // 2
    me_a, me_t = lax.axis_index("adapter"), lax.axis_index("tensor")
    z, core = lax.div(me_a, 2), lax.rem(me_a, 2)
    y, x = lax.div(me_t, nx), lax.rem(me_t, nx)

    barrier = pltpu.get_barrier_semaphore()
    for to in (lax.rem(z + 1, nz) * 2 + core, lax.rem(z + nz - 1, nz) * 2 + core, z * 2 + 1 - core):
        pl.semaphore_signal(barrier, inc=1, device_id={"adapter": to}, device_id_type=MESH)

    def greet(d, carry):
        to = lax.rem(me_t + d, tensors)
        pl.semaphore_signal(barrier, inc=1, device_id={"tensor": to}, device_id_type=MESH)
        return carry

    lax.fori_loop(1, tensors, greet, 0)
    w_in = pltpu.make_async_copy(w_hbm, wv, in_sem.at[0])
    x_in = pltpu.make_async_copy(x_hbm, xv, in_sem.at[1])
    w_in.start()
    x_in.start()
    for j in range(ACTIVE):
        pk[j] = down_ref[idx[j]]
        pk[ACTIVE + j] = up_ref[idx[j]]
    pl.semaphore_wait(barrier, tensors + 2)

    panels = RingGather(nz, z, core, pk, ga, gs_a, gr_a, gp_a, own_sem.at[0])
    parts = RingGather(nz, z, core, gk, gb, gs_b, gr_b, gp_b, own_sem.at[1])
    along_x = lambda place: y * nx + place
    along_y = lambda place: place * nx + x
    sum_x1 = RingSum(nx, x, along_x, f1, r1, s_r1, v_r1)
    sum_y1 = RingSum(ny, y, along_y, f2, r2, s_r2, v_r2)
    sum_y2 = RingSum(ny, y, along_y, s1, q1, s_q1, v_q1)
    sum_x2 = RingSum(nx, x, along_x, s2, q2, s_q2, v_q2)

    panels.start()
    w_in.wait()

    def frozen_term(t, carry):
        term = dot(g_ref[...], wv[t], 1, 1).astype(BF16)
        ty, tx = lax.div(t, nx), lax.rem(t, nx)
        f1[tx, lax.div(ty, hy), lax.rem(ty, hy)] = term[:SEG_ROWS]
        f2[ty, lax.div(tx, hx), lax.rem(tx, hx)] = term[SEG_ROWS:]
        return carry

    lax.fori_loop(0, tensors, frozen_term, 0)
    sum_x1.start()
    sum_y1.start()
    panels.step(0)
    order = []
    for k in range(1, max(panels.steps, sum_y1.steps)):
        order += [(sum_y1, k - 1), (sum_x1, k - 1), (panels, k)]
    for ring, k in order:
        if k < ring.steps:
            ring.step(k)
    panels.finish()

    x_in.wait()
    col0 = pl.multiple_of(me_t * COLS, COLS)
    for s in range(2):
        rows = slice(s * SEG_ROWS, (s + 1) * SEG_ROWS)
        low = dot(xv[rows, pl.ds(col0, COLS)], ga[idx[2 + s]], 1, 1)
        back = dot(g_ref[rows, :], ga[idx[2 + s] + ACTIVE], 1, 1)
        both = jnp.concatenate([low, back], axis=1)
        per = tensors // 2
        part[s * per:(s + 1) * per] = both.reshape(per, SEG_ROWS // per, 2 * RANK)

    def to_peer(src, dst, phase, d):
        return pltpu.make_async_remote_copy(
            src_ref=src, dst_ref=dst, send_sem=ar_send.at[phase], recv_sem=ar_recv.at[phase],
            device_id={"tensor": lax.rem(me_t + d, tensors)}, device_id_type=MESH,
        )

    def scatter(d, carry):
        to_peer(part.at[lax.rem(me_t + d, tensors)], inbox.at[d - 1], 0, d).start()
        return carry

    lax.fori_loop(1, tensors, scatter, 0)

    acc[...] = jnp.zeros_like(acc)

    def forward(k, carry):
        at = pl.multiple_of(k * COLS, COLS)
        acc[...] += dot(xv[:, pl.ds(at, COLS)], wv[k], 1, 0)
        return carry

    lax.fori_loop(0, tensors, forward, 0)

    others = inbox.at[pl.ds(0, tensors - 1)]
    to_peer(others, others, 0, 1).wait_recv()
    value = part[me_t]
    for d in range(tensors - 1):
        value = value + inbox[d]
    mine[...] = value
    total[me_t] = value

    def spread(d, carry):
        to_peer(mine, total.at[me_t], 1, d).start()
        return carry

    lax.fori_loop(1, tensors, spread, 0)

    sum_x1.finish()
    sum_y1.finish()
    for h in range(2):
        def first_x(j, carry):
            v = sum_x1.total(h, j).astype(BF16)
            s1[h * hy + j, 0] = v[:RANK]
            s1[h * hy + j, 1] = v[RANK:]
            return carry

        def first_y(j, carry):
            v = sum_y1.total(h, j).astype(BF16)
            s2[h * hx + j, 0] = v[:RANK]
            s2[h * hx + j, 1] = v[RANK:]
            return carry

        lax.fori_loop(0, hy, first_x, 0)
        lax.fori_loop(0, hx, first_y, 0)
    rest = total.at[pl.ds(0, tensors - 1)]
    to_peer(rest, rest, 1, 1).wait_recv()

    ranks = total[...].reshape(2 * SEG_ROWS, 2 * RANK)
    halves, downs, ups = [], [], []
    for s in range(2):
        rows = slice(s * SEG_ROWS, (s + 1) * SEG_ROWS)
        low_half = ranks[rows, :RANK].astype(BF16)
        back_half = (adapter_scale * ranks[rows, RANK:]).astype(BF16)
        halves.append((low_half, back_half))
        downs.append(dot(back_half, xv[rows, pl.ds(col0, COLS)], 0, 0))
        ups.append(adapter_scale * dot(low_half, g_ref[rows, :], 0, 0))
    same = mask[0]
    for base, terms in ((0, downs), (ACTIVE, ups)):
        gk[base] = (terms[0] + same * terms[1]).astype(BF16)
        gk[base + 1] = ((1.0 - same) * terms[1]).astype(BF16)
    parts.start()
    sum_y2.start()
    sum_x2.start()
    for s in range(2):
        rows = slice(s * SEG_ROWS, (s + 1) * SEG_ROWS)
        low_half, back_half = halves[s]
        adapted = dot(low_half, ga[idx[2 + s] + ACTIVE], 1, 0)
        po_ref[rows, :] = (acc[rows, :] + adapter_scale * adapted).astype(BF16)
        acc[rows, :] = dot(back_half, ga[idx[2 + s]], 1, 0)
    for k in range(max(parts.steps, sum_y2.steps)):
        for ring in (parts, sum_y2, sum_x2):
            if k < ring.steps:
                ring.step(k)
        if k == sum_y2.steps - 1:
            sum_y2.finish()
            sum_x2.finish()
            for s, ring in ((0, sum_y2), (1, sum_x2)):
                for h in range(2):
                    rows = slice(s * SEG_ROWS + h * RANK, s * SEG_ROWS + (h + 1) * RANK)
                    gi_ref[rows, :] = (ring.total(h) + acc[rows, :]).astype(BF16)
    parts.finish()

    segs = owners * ACTIVE
    for base, out in ((0, dg_ref), (ACTIVE, ug_ref)):
        def gather(i, carry):
            g, s = lax.div(i, 2), lax.rem(i, 2)
            block = gb[g * 4 + base + s].astype(F32)
            return carry[0] + mask[1 + i] * block, carry[1] + mask[1 + segs + i] * block

        zero = jnp.zeros((RANK, COLS), F32)
        first, second = lax.fori_loop(0, segs, gather, (zero, zero))

        def place(i, carry):
            at = 1 + 2 * segs + i
            out[i] = (mask[at] * first + mask[at + ADP_OWN] * second).astype(BF16)
            return carry

        lax.fori_loop(0, ADP_OWN, place, 0)

    panels.drain()
    parts.drain()
    for ring in (sum_x1, sum_y1, sum_y2, sum_x2):
        ring.drain()
    to_peer(others, others, 0, 1).wait_send()
    to_peer(others, others, 1, 1).wait_send()


def per_device(
    rollout_activations,
    projection_weight,
    adapter_down_panels,
    adapter_up_panels,
    output_gradient,
    segment_adapter,
):
    owners, tensors = lax.axis_size("adapter"), lax.axis_size("tensor")
    nz, nx = owners // 2, X_CHIPS
    ny = tensors // nx
    me = lax.axis_index("adapter")
    all_ids = jnp.arange(owners * ADP_OWN, dtype=jnp.int32)
    use = jnp.any(segment_adapter[:, None] == all_ids[None, :], axis=0)
    grid = use.reshape(owners, ADP_OWN).astype(jnp.int32)
    rank = jnp.cumsum(grid, axis=1) - 1
    group_ids = lax.dynamic_slice_in_dim(segment_adapter, me * 2, 2)
    slot = jnp.sum(
        jnp.where(group_ids[:, None] == all_ids[None, :], rank.reshape(1, -1), 0), axis=1
    )
    own_use = lax.dynamic_index_in_dim(grid, me, 0, keepdims=False)
    own_rank = lax.dynamic_index_in_dim(rank, me, 0, keepdims=False)
    picker = (own_rank[None, :] == jnp.arange(ACTIVE, dtype=jnp.int32)[:, None]) & (
        own_use[None, :] > 0
    )
    own_local = jnp.sum(jnp.where(picker, jnp.arange(ADP_OWN, dtype=jnp.int32)[None, :], 0), axis=1)
    idx = jnp.concatenate([own_local, (group_ids // ADP_OWN) * 4 + slot]).astype(jnp.int32)
    own_named = jnp.any(picker, axis=1)
    named = own_named[:, None] & (segment_adapter[None, :] == (me * ADP_OWN + own_local)[:, None])
    same = (group_ids[0] == group_ids[1]).reshape(1)
    mask = jnp.concatenate([same, named.reshape(-1), picker.reshape(-1)]).astype(F32)

    rows, width = rollout_activations.shape
    blocks = owners * 4
    slots_x, slots_y = chains_of(nx)[1], chains_of(ny)[1]
    vmem = pltpu.VMEM
    dma, block = pltpu.SemaphoreType.DMA, (RANK, COLS)
    gather_sems = [dma(()), dma((2, nz // 2, 2)), dma(())]
    seg = (SEG_ROWS, COLS)
    scratch = [
        vmem((rows, width), BF16),
        vmem((tensors, COLS, COLS), BF16),
        vmem((rows, COLS), F32),
        vmem((4,) + block, BF16),
        vmem((blocks,) + block, BF16),
        vmem((4,) + block, BF16),
        vmem((blocks,) + block, BF16),
        vmem((nx, 2, ny // 2) + seg, BF16),
        vmem((ny, 2, nx // 2) + seg, BF16),
        vmem((slots_x, ny // 2) + seg, BF16),
        vmem((slots_y, nx // 2) + seg, BF16),
        vmem((ny, 2) + block, BF16),
        vmem((nx, 2) + block, BF16),
        vmem((slots_y,) + block, BF16),
        vmem((slots_x,) + block, BF16),
        vmem((tensors, rows // tensors, 2 * RANK), F32),
        vmem((tensors, rows // tensors, 2 * RANK), F32),
        vmem((rows // tensors, 2 * RANK), F32),
        vmem((tensors, rows // tensors, 2 * RANK), F32),
        dma((2,)),
        dma((2,)),
        *gather_sems,
        *gather_sems,
    ]
    for slots in (slots_x, slots_y, slots_y, slots_x):
        scratch += [dma(()), dma((slots,))]
    scratch += [dma((2,)), dma((2,))]
    smem, whole, any_space = (
        pl.BlockSpec(memory_space=pltpu.SMEM),
        pl.BlockSpec(memory_space=pltpu.VMEM),
        pl.BlockSpec(memory_space=pl.ANY),
    )
    out = [
        jax.ShapeDtypeStruct((rows, COLS), BF16),
        jax.ShapeDtypeStruct((rows, COLS), BF16),
        jax.ShapeDtypeStruct((ADP_OWN,) + block, BF16),
        jax.ShapeDtypeStruct((ADP_OWN,) + block, BF16),
    ]
    return tuple(
        pl.pallas_call(
            functools.partial(step_kernel, owners, tensors),
            out_shape=out,
            in_specs=[smem, smem, any_space, any_space, whole, whole, whole],
            out_specs=[whole] * 4,
            scratch_shapes=scratch,
            compiler_params=pltpu.CompilerParams(
                collective_id=0, has_side_effects=True, vmem_limit_bytes=60 * 1024 * 1024
            ),
        )(
            idx,
            mask,
            rollout_activations,
            projection_weight.reshape(tensors, COLS, COLS),
            adapter_down_panels,
            adapter_up_panels,
            output_gradient,
        )
    )


def solution(mesh):
    in_specs = (
        P("adapter", None),
        P(None, "tensor"),
        P("adapter", None, "tensor"),
        P("adapter", None, "tensor"),
        P("adapter", "tensor"),
        P(),
    )
    out_specs = (
        P("adapter", "tensor"),
        P("adapter", "tensor"),
        P("adapter", None, "tensor"),
        P("adapter", None, "tensor"),
    )
    return jax.shard_map(
        per_device, mesh=mesh, in_specs=in_specs, out_specs=out_specs, check_vma=False
    )
```

```python
import functools

import jax
import jax.numpy as jnp
from jax import lax
from jax.experimental import pallas as pl
from jax.experimental.pallas import tpu as pltpu
from jax.sharding import PartitionSpec as P

SEG_ROWS = 128
ADP_OWN = 16
ACTIVE = 2
RANK = 64
COLS = 256
X_CHIPS = 4
MESH = pl.DeviceIdType.MESH
F32 = jnp.float32
BF16 = jnp.bfloat16

adapter_scale = 0.5


def dot(a, b, ca, cb):
    return lax.dot_general(a, b, (((ca,), (cb,)), ((), ())), preferred_element_type=F32)


def chains_of(n):
    half = n // 2
    chains, base = [], 0
    for sign, part, length in ((1, 0, half), (-1, 1, half), (1, 1, half - 1), (-1, 0, half - 1)):
        if length:
            chains.append((sign, part, length, base))
            base += length
    return chains, base


class RingSum:
    def __init__(self, n, pos, device_of, src, land, send_sem, recv_sem):
        self.n, self.pos, self.device_of = n, pos, device_of
        self.src, self.land, self.send_sem, self.recv_sem = src, land, send_sem, recv_sem
        self.chains, _ = chains_of(n)
        self.steps = n // 2

    def at(self, offset):
        return lax.rem(self.pos + offset + self.n, self.n)

    def copy(self, src, slot, sign):
        return pltpu.make_async_remote_copy(
            src_ref=src,
            dst_ref=self.land.at[slot],
            send_sem=self.send_sem,
            recv_sem=self.recv_sem.at[slot],
            device_id={"tensor": self.device_of(self.at(sign))},
            device_id_type=MESH,
        )

    def start(self):
        for sign, part, length, base in self.chains:
            self.copy(self.src.at[self.at(sign * length), part], base, sign).start()

    def step(self, s):
        for sign, part, length, base in self.chains:
            if s >= length - 1:
                continue
            slot = base + s
            self.copy(self.land.at[slot], slot, sign).wait_recv()
            place = self.at(sign * (length - s - 1))
            self.add(slot, place, part)
            self.copy(self.land.at[slot], slot + 1, sign).start()

    def add(self, slot, place, part):
        if len(self.land.shape) == 3:
            total = self.land[slot].astype(F32) + self.src[place, part].astype(F32)
            self.land[slot] = total.astype(BF16)
            return

        def body(j, carry):
            total = self.land[slot, j].astype(F32) + self.src[place, part, j].astype(F32)
            self.land[slot, j] = total.astype(BF16)
            return carry

        lax.fori_loop(0, self.land.shape[1], body, 0)

    def finish(self):
        for sign, part, length, base in self.chains:
            slot = base + length - 1
            self.copy(self.land.at[slot], slot, sign).wait_recv()

    def lasts(self, part):
        return [base + length - 1 for _, p, length, base in self.chains if p == part]

    def total(self, part, *index):
        value = self.src[(self.pos, part) + index].astype(F32)
        for slot in self.lasts(part):
            value = value + self.land[(slot,) + index].astype(F32)
        return value

    def drain(self):
        whole = self.src.at[pl.ds(0, self.n - 1)]
        pltpu.make_async_remote_copy(
            src_ref=whole,
            dst_ref=whole,
            send_sem=self.send_sem,
            recv_sem=self.recv_sem.at[0],
            device_id={"tensor": self.device_of(self.at(1))},
            device_id_type=MESH,
        ).wait_send()


class RingGather:
    def __init__(self, n, z, core, own, out, send_sem, recv_sem, pair_sem, own_sem):
        self.n, self.z, self.core = n, z, core
        self.own, self.out = own, out
        self.send_sem, self.recv_sem, self.pair_sem, self.own_sem = send_sem, recv_sem, pair_sem, own_sem
        self.steps = n // 2

    def has(self, d, k, ch):
        return k < self.steps - 1 or (k == self.steps - 1 and d == ch)

    def rows(self, z, core, ch):
        return self.out.at[pl.ds((z * 2 + core) * 4 + ch * 2, 2)]

    def ring(self, src, dst, d, k, ch):
        sign = 1 - 2 * d
        z_to = lax.rem(self.z + sign + self.n, self.n)
        return pltpu.make_async_remote_copy(
            src_ref=src,
            dst_ref=dst,
            send_sem=self.send_sem,
            recv_sem=self.recv_sem.at[d, k, ch],
            device_id={"adapter": z_to * 2 + self.core},
            device_id_type=MESH,
        )

    def pair(self, src, dst, k):
        return pltpu.make_async_remote_copy(
            src_ref=src,
            dst_ref=dst,
            send_sem=self.send_sem,
            recv_sem=self.pair_sem.at[k],
            device_id={"adapter": self.z * 2 + 1 - self.core},
            device_id_type=MESH,
        )

    def own_copy(self):
        return pltpu.make_async_copy(
            self.own, self.out.at[pl.ds((self.z * 2 + self.core) * 4, 4)], self.own_sem
        )

    def start(self):
        for ch in range(2):
            src, dst = self.own.at[pl.ds(ch * 2, 2)], self.rows(self.z, self.core, ch)
            for d in range(2):
                if self.has(d, 0, ch):
                    self.ring(src, dst, d, 0, ch).start()
        for ch in range(2):
            src, dst = self.own.at[pl.ds(ch * 2, 2)], self.rows(self.z, self.core, ch)
            self.pair(src, dst, 0).start()
        self.own_copy().start()

    def step(self, k):
        for ch in range(2):
            for d in range(2):
                if not self.has(d, k, ch):
                    continue
                sign = 1 - 2 * d
                z_from = lax.rem(self.z - sign * (k + 1) + 2 * self.n, self.n)
                block = self.rows(z_from, self.core, ch)
                self.ring(block, block, d, k, ch).wait_recv()
                if self.has(d, k + 1, ch):
                    self.ring(block, block, d, k + 1, ch).start()
                self.pair(block, block, k + 1).start()

    def pair_wait(self, k):
        count = 2 if k == 0 else sum(self.has(d, k - 1, ch) for d in range(2) for ch in range(2))
        landed = self.out.at[pl.ds(0, 2 * count)]
        self.pair(landed, landed, k).wait_recv()

    def places(self, k):
        return [self.z] if k == 0 else [
            lax.rem(self.z + sign * k + self.n, self.n) for sign in ((1, -1) if k < self.steps else (1,))
        ]

    def drain(self):
        sent = self.out.at[pl.ds(0, (4 * self.n - 2) * 2)]
        self.pair(sent, sent, 0).wait_send()


def named_range(ids, segs, owner):
    start = owner * ADP_OWN

    def body(i, carry):
        low, high = carry
        v = ids[i]
        held = (v >= start) & (v < start + ADP_OWN)
        return (
            jnp.where(held, jnp.minimum(low, v), low),
            jnp.where(held, jnp.maximum(high, v), high),
        )

    return lax.fori_loop(0, segs, body, (start + ADP_OWN, start - 1))


def step_kernel(
    owners, tensors,
    ids, x_hbm, w_hbm, down_ref, up_ref, g_ref,
    po_ref, gi_ref, sums_ref,
    asum, xv, wv, acc, pk, ga, gk, gb, f1, f2, r1, r2, s1, s2, q1, q2, part, inbox, mine, total,
    in_sem, own_sem, gs_a, gr_a, gp_a, gs_b, gr_b, gp_b,
    s_r1, v_r1, s_r2, v_r2, s_q1, v_q1, s_q2, v_q2, ar_send, ar_recv,
):
    nz, nx = owners // 2, X_CHIPS
    ny = tensors // nx
    hx, hy = nx // 2, ny // 2
    me_a, me_t = lax.axis_index("adapter"), lax.axis_index("tensor")
    z, core = lax.div(me_a, 2), lax.rem(me_a, 2)
    y, x = lax.div(me_t, nx), lax.rem(me_t, nx)

    barrier = pltpu.get_barrier_semaphore()
    for to in (lax.rem(z + 1, nz) * 2 + core, lax.rem(z + nz - 1, nz) * 2 + core, z * 2 + 1 - core):
        pl.semaphore_signal(barrier, inc=1, device_id={"adapter": to}, device_id_type=MESH)

    def greet(d, carry):
        to = lax.rem(me_t + d, tensors)
        pl.semaphore_signal(barrier, inc=1, device_id={"tensor": to}, device_id_type=MESH)
        return carry

    lax.fori_loop(1, tensors, greet, 0)
    w_in = pltpu.make_async_copy(w_hbm, wv, in_sem.at[0])
    x_in = pltpu.make_async_copy(x_hbm, xv, in_sem.at[1])
    w_in.start()
    x_in.start()
    segs = owners * 2
    own_low, own_high = named_range(ids, segs, me_a)
    for j, v in enumerate((own_low, own_high)):
        local = jnp.clip(v - me_a * ADP_OWN, 0, ADP_OWN - 1)
        pk[j] = down_ref[local]
        pk[ACTIVE + j] = up_ref[local]

    panels = RingGather(nz, z, core, pk, ga, gs_a, gr_a, gp_a, own_sem.at[0])
    parts = RingGather(nz, z, core, gk, gb, gs_b, gr_b, gp_b, own_sem.at[1])
    along_x = lambda place: y * nx + place
    along_y = lambda place: place * nx + x
    sum_x1 = RingSum(nx, x, along_x, f1, r1, s_r1, v_r1)
    sum_y1 = RingSum(ny, y, along_y, f2, r2, s_r2, v_r2)
    sum_y2 = RingSum(ny, y, along_y, s1, q1, s_q1, v_q1)
    sum_x2 = RingSum(nx, x, along_x, s2, q2, s_q2, v_q2)

    w_in.wait()

    def frozen_term(t, carry):
        term = dot(g_ref[...], wv[t], 1, 1).astype(BF16)
        ty, tx = lax.div(t, nx), lax.rem(t, nx)
        f1[tx, lax.div(ty, hy), lax.rem(ty, hy)] = term[:SEG_ROWS]
        f2[ty, lax.div(tx, hx), lax.rem(tx, hx)] = term[SEG_ROWS:]
        return carry

    lax.fori_loop(0, tensors, frozen_term, 0)
    pl.semaphore_wait(barrier, tensors + 2)
    panels.start()
    sum_x1.start()
    sum_y1.start()
    seg_block = []
    for s in range(2):
        v = ids[me_a * 2 + s]
        owner = lax.div(v, ADP_OWN)
        low, _ = named_range(ids, segs, owner)
        seg_block.append(owner * 4 + jnp.where(v > low, 1, 0))
    same = jnp.where(ids[me_a * 2] == ids[me_a * 2 + 1], 1.0, 0.0).astype(F32)
    asum[...] = jnp.zeros_like(asum)
    order = [(panels, 0), (panels, 1), (sum_y1, 0), (sum_x1, 0), (panels, 2), (panels, 3), (panels, 4), (sum_y1, 1)]
    order += [(panels, k) for k in range(5, panels.steps)]
    for ring, k in order:
        if k < ring.steps:
            ring.step(k)
    panels.own_copy().wait()
    for k in range(panels.steps + 1):
        panels.pair_wait(k)

    x_in.wait()
    col0 = pl.multiple_of(me_t * COLS, COLS)
    for s in range(2):
        rows = slice(s * SEG_ROWS, (s + 1) * SEG_ROWS)
        low = dot(xv[rows, pl.ds(col0, COLS)], ga[seg_block[s]], 1, 1)
        back = dot(g_ref[rows, :], ga[seg_block[s] + ACTIVE], 1, 1)
        both = jnp.concatenate([low, back], axis=1)
        per = tensors // 2
        part[s * per:(s + 1) * per] = both.reshape(per, SEG_ROWS // per, 2 * RANK)

    def to_peer(src, dst, phase, d):
        return pltpu.make_async_remote_copy(
            src_ref=src, dst_ref=dst, send_sem=ar_send.at[phase], recv_sem=ar_recv.at[phase],
            device_id={"tensor": lax.rem(me_t + d, tensors)}, device_id_type=MESH,
        )

    def scatter(d, carry):
        to_peer(part.at[lax.rem(me_t + d, tensors)], inbox.at[d - 1], 0, d).start()
        return carry

    lax.fori_loop(1, tensors, scatter, 0)

    acc[...] = jnp.zeros_like(acc)

    def forward(k, carry):
        at = pl.multiple_of(k * COLS, COLS)
        acc[...] += dot(xv[:, pl.ds(at, COLS)], wv[k], 1, 0)
        return carry

    lax.fori_loop(0, tensors, forward, 0)

    others = inbox.at[pl.ds(0, tensors - 1)]
    to_peer(others, others, 0, 1).wait_recv()
    value = part[me_t]
    for d in range(tensors - 1):
        value = value + inbox[d]
    mine[...] = value
    total[me_t] = value

    def spread(d, carry):
        to_peer(mine, total.at[me_t], 1, d).start()
        return carry

    lax.fori_loop(1, tensors, spread, 0)

    for k in range(2, sum_y1.steps):
        sum_y1.step(k)
    sum_x1.finish()
    for h in range(2):
        def first_x(j, carry):
            v = sum_x1.total(h, j).astype(BF16)
            s1[h * hy + j, 0] = v[:RANK]
            s1[h * hy + j, 1] = v[RANK:]
            return carry

        lax.fori_loop(0, hy, first_x, 0)
    rest = total.at[pl.ds(0, tensors - 1)]
    to_peer(rest, rest, 1, 1).wait_recv()

    ranks = total[...].reshape(2 * SEG_ROWS, 2 * RANK)
    halves, downs, ups = [], [], []
    for s in range(2):
        rows = slice(s * SEG_ROWS, (s + 1) * SEG_ROWS)
        low_half = ranks[rows, :RANK].astype(BF16)
        back_half = (adapter_scale * ranks[rows, RANK:]).astype(BF16)
        halves.append((low_half, back_half))
        downs.append(dot(back_half, xv[rows, pl.ds(col0, COLS)], 0, 0))
        ups.append(adapter_scale * dot(low_half, g_ref[rows, :], 0, 0))
    for base, terms in ((0, downs), (ACTIVE, ups)):
        gk[base] = (terms[0] + same * terms[1]).astype(BF16)
        gk[base + 1] = ((1.0 - same) * terms[1]).astype(BF16)
    parts.start()
    sum_y2.start()
    for s in range(2):
        rows = slice(s * SEG_ROWS, (s + 1) * SEG_ROWS)
        low_half, back_half = halves[s]
        adapted = dot(low_half, ga[seg_block[s] + ACTIVE], 1, 0)
        po_ref[rows, :] = (acc[rows, :] + adapter_scale * adapted).astype(BF16)
        acc[rows, :] = dot(back_half, ga[seg_block[s]], 1, 0)

    def add_group(place, side):
        group = place * 2 + side
        for slot, v in enumerate((own_low, own_high)):
            hits = []
            for s in range(2):
                hit = ids[group * 2 + s] == v
                if slot:
                    hit = hit & (own_high != own_low)
                hits.append(jnp.where(hit, 1.0, 0.0).astype(F32))
            for du in range(2):
                at = group * 4 + du * 2
                asum[du * 2 + slot] += hits[0] * gb[at].astype(F32) + hits[1] * gb[at + 1].astype(F32)

    def add_side(k, side):
        for place in parts.places(k):
            add_group(place, side)

    def finish_y1():
        sum_y1.finish()
        for h in range(2):
            def first_y(j, carry):
                v = sum_y1.total(h, j).astype(BF16)
                s2[h * hx + j, 0] = v[:RANK]
                s2[h * hx + j, 1] = v[RANK:]
                return carry

            lax.fori_loop(0, hx, first_y, 0)
        sum_x2.start()

    def finish_frozen():
        sum_y2.finish()
        sum_x2.finish()
        for s, ring in ((0, sum_y2), (1, sum_x2)):
            for h in range(2):
                rows = slice(s * SEG_ROWS + h * RANK, s * SEG_ROWS + (h + 1) * RANK)
                gi_ref[rows, :] = (ring.total(h) + acc[rows, :]).astype(BF16)

    for k in range(max(parts.steps, sum_y2.steps)):
        if k < parts.steps:
            parts.step(k)
        if k == 0:
            finish_y1()
            parts.own_copy().wait()
            add_side(0, core)
        for ring, j in ((sum_y2, k), (sum_x2, k - 1)):
            if 0 <= j < ring.steps:
                ring.step(j)
        if k < parts.steps:
            parts.pair_wait(k)
            add_side(k, 1 - core)
            add_side(k + 1, core)
        if k == max(sum_y2.steps, sum_x2.steps + 1) - 1:
            finish_frozen()
    parts.pair_wait(parts.steps)
    add_side(parts.steps, 1 - core)
    sums_ref[...] = asum[...].astype(BF16)

    panels.drain()
    parts.drain()
    for ring in (sum_x1, sum_y1, sum_y2, sum_x2):
        ring.drain()
    to_peer(others, others, 0, 1).wait_send()
    to_peer(others, others, 1, 1).wait_send()


def place_kernel(segs, ids, po_in, gi_in, sums, po_ref, gi_ref, dg_ref, ug_ref):
    start = lax.axis_index("adapter") * ADP_OWN
    low, high = named_range(ids, segs, lax.axis_index("adapter"))
    po_ref[...] = po_in[...]
    gi_ref[...] = gi_in[...]
    for base, out in ((0, dg_ref), (ACTIVE, ug_ref)):
        def place(i, carry):
            first = jnp.where(start + i == low, 1.0, 0.0).astype(F32)
            second = jnp.where((start + i == high) & (high != low), 1.0, 0.0).astype(F32)
            out[i] = (first * sums[base].astype(F32) + second * sums[base + 1].astype(F32)).astype(BF16)
            return carry

        lax.fori_loop(0, ADP_OWN, place, 0)


def per_device(
    rollout_activations,
    projection_weight,
    adapter_down_panels,
    adapter_up_panels,
    output_gradient,
    segment_adapter,
):
    owners, tensors = lax.axis_size("adapter"), lax.axis_size("tensor")
    nz, nx = owners // 2, X_CHIPS
    ny = tensors // nx
    rows, width = rollout_activations.shape
    blocks = owners * 4
    slots_x, slots_y = chains_of(nx)[1], chains_of(ny)[1]
    vmem = pltpu.VMEM
    dma, block = pltpu.SemaphoreType.DMA, (RANK, COLS)
    gather_sems = [dma(()), dma((2, nz // 2, 2)), dma((nz // 2 + 1,))]
    seg = (SEG_ROWS, COLS)
    scratch = [
        vmem((4,) + block, F32),
        vmem((rows, width), BF16),
        vmem((tensors, COLS, COLS), BF16),
        vmem((rows, COLS), F32),
        vmem((4,) + block, BF16),
        vmem((blocks,) + block, BF16),
        vmem((4,) + block, BF16),
        vmem((blocks,) + block, BF16),
        vmem((nx, 2, ny // 2) + seg, BF16),
        vmem((ny, 2, nx // 2) + seg, BF16),
        vmem((slots_x, ny // 2) + seg, BF16),
        vmem((slots_y, nx // 2) + seg, BF16),
        vmem((ny, 2) + block, BF16),
        vmem((nx, 2) + block, BF16),
        vmem((slots_y,) + block, BF16),
        vmem((slots_x,) + block, BF16),
        vmem((tensors, rows // tensors, 2 * RANK), F32),
        vmem((tensors, rows // tensors, 2 * RANK), F32),
        vmem((rows // tensors, 2 * RANK), F32),
        vmem((tensors, rows // tensors, 2 * RANK), F32),
        dma((2,)),
        dma((2,)),
        *gather_sems,
        *gather_sems,
    ]
    for slots in (slots_x, slots_y, slots_y, slots_x):
        scratch += [dma(()), dma((slots,))]
    scratch += [dma((2,)), dma((2,))]
    smem, whole, any_space = (
        pl.BlockSpec(memory_space=pltpu.SMEM),
        pl.BlockSpec(memory_space=pltpu.VMEM),
        pl.BlockSpec(memory_space=pl.ANY),
    )
    like_rows = jax.ShapeDtypeStruct((rows, COLS), BF16)
    like_panels = jax.ShapeDtypeStruct((ADP_OWN,) + block, BF16)
    po, gi, sums = pl.pallas_call(
        functools.partial(step_kernel, owners, tensors),
        out_shape=[like_rows, like_rows, jax.ShapeDtypeStruct((4,) + block, BF16)],
        in_specs=[smem, any_space, any_space, whole, whole, whole],
        out_specs=[whole] * 3,
        scratch_shapes=scratch,
        compiler_params=pltpu.CompilerParams(
            collective_id=0, has_side_effects=True, vmem_limit_bytes=60 * 1024 * 1024
        ),
    )(
        segment_adapter,
        rollout_activations,
        projection_weight.reshape(tensors, COLS, COLS),
        adapter_down_panels,
        adapter_up_panels,
        output_gradient,
    )
    return tuple(
        pl.pallas_call(
            functools.partial(place_kernel, owners * 2),
            out_shape=[like_rows, like_rows, like_panels, like_panels],
            in_specs=[smem, whole, whole, whole],
            out_specs=[whole] * 4,
        )(segment_adapter, po, gi, sums)
    )


def solution(mesh):
    in_specs = (
        P("adapter", None),
        P(None, "tensor"),
        P("adapter", None, "tensor"),
        P("adapter", None, "tensor"),
        P("adapter", "tensor"),
        P(),
    )
    out_specs = (
        P("adapter", "tensor"),
        P("adapter", "tensor"),
        P("adapter", None, "tensor"),
        P("adapter", None, "tensor"),
    )
    return jax.shard_map(
        per_device, mesh=mesh, in_specs=in_specs, out_specs=out_specs, check_vma=False
    )
```

```python
import functools

import jax
import jax.numpy as jnp
from jax import lax
from jax.experimental import pallas as pl
from jax.experimental.pallas import tpu as pltpu
from jax.sharding import PartitionSpec as P

SEG_ROWS = 128
ADP_OWN = 16
ACTIVE = 2
RANK = 64
COLS = 256
X_CHIPS = 4
MESH = pl.DeviceIdType.MESH
F32 = jnp.float32
BF16 = jnp.bfloat16

adapter_scale = 0.5


def dot(a, b, ca, cb):
    return lax.dot_general(a, b, (((ca,), (cb,)), ((), ())), preferred_element_type=F32)


def chains_of(n):
    half = n // 2
    chains, base = [], 0
    for sign, part, length in ((1, 0, half), (-1, 1, half), (1, 1, half - 1), (-1, 0, half - 1)):
        if length:
            chains.append((sign, part, length, base))
            base += length
    return chains, base


class RingSum:
    def __init__(self, n, pos, device_of, src, land, send_sem, recv_sem):
        self.n, self.pos, self.device_of = n, pos, device_of
        self.src, self.land, self.send_sem, self.recv_sem = src, land, send_sem, recv_sem
        self.chains, _ = chains_of(n)
        self.steps = n // 2

    def at(self, offset):
        return lax.rem(self.pos + offset + self.n, self.n)

    def copy(self, src, slot, sign):
        return pltpu.make_async_remote_copy(
            src_ref=src,
            dst_ref=self.land.at[slot],
            send_sem=self.send_sem,
            recv_sem=self.recv_sem.at[slot],
            device_id={"tensor": self.device_of(self.at(sign))},
            device_id_type=MESH,
        )

    def start(self):
        for sign, part, length, base in self.chains:
            self.copy(self.src.at[self.at(sign * length), part], base, sign).start()

    def step(self, s):
        for sign, part, length, base in self.chains:
            if s >= length - 1:
                continue
            slot = base + s
            self.copy(self.land.at[slot], slot, sign).wait_recv()
            place = self.at(sign * (length - s - 1))
            self.add(slot, place, part)
            self.copy(self.land.at[slot], slot + 1, sign).start()

    def add(self, slot, place, part):
        if len(self.land.shape) == 3:
            total = self.land[slot].astype(F32) + self.src[place, part].astype(F32)
            self.land[slot] = total.astype(BF16)
            return

        def body(j, carry):
            total = self.land[slot, j].astype(F32) + self.src[place, part, j].astype(F32)
            self.land[slot, j] = total.astype(BF16)
            return carry

        lax.fori_loop(0, self.land.shape[1], body, 0)

    def finish(self):
        for sign, part, length, base in self.chains:
            slot = base + length - 1
            self.copy(self.land.at[slot], slot, sign).wait_recv()

    def lasts(self, part):
        return [base + length - 1 for _, p, length, base in self.chains if p == part]

    def total(self, part, *index):
        value = self.src[(self.pos, part) + index].astype(F32)
        for slot in self.lasts(part):
            value = value + self.land[(slot,) + index].astype(F32)
        return value

    def drain(self):
        whole = self.src.at[pl.ds(0, self.n - 1)]
        pltpu.make_async_remote_copy(
            src_ref=whole,
            dst_ref=whole,
            send_sem=self.send_sem,
            recv_sem=self.recv_sem.at[0],
            device_id={"tensor": self.device_of(self.at(1))},
            device_id_type=MESH,
        ).wait_send()


class RingGather:
    def __init__(self, n, z, core, own, out, send_sem, recv_sem, pair_sem, own_sem):
        self.n, self.z, self.core = n, z, core
        self.own, self.out = own, out
        self.send_sem, self.recv_sem, self.pair_sem, self.own_sem = send_sem, recv_sem, pair_sem, own_sem
        self.steps = n // 2

    def has(self, d, k, ch):
        return k < self.steps - 1 or (k == self.steps - 1 and d == ch // 2)

    def rows(self, z, core, ch, count=1):
        return self.out.at[pl.ds((z * 2 + core) * 4 + ch, count)]

    def ring(self, src, dst, d, k, ch):
        sign = 1 - 2 * d
        z_to = lax.rem(self.z + sign + self.n, self.n)
        return pltpu.make_async_remote_copy(
            src_ref=src,
            dst_ref=dst,
            send_sem=self.send_sem,
            recv_sem=self.recv_sem.at[d, k, ch],
            device_id={"adapter": z_to * 2 + self.core},
            device_id_type=MESH,
        )

    def pair(self, src, dst, k):
        return pltpu.make_async_remote_copy(
            src_ref=src,
            dst_ref=dst,
            send_sem=self.send_sem,
            recv_sem=self.pair_sem.at[k],
            device_id={"adapter": self.z * 2 + 1 - self.core},
            device_id_type=MESH,
        )

    def own_copy(self):
        return pltpu.make_async_copy(
            self.own, self.out.at[pl.ds((self.z * 2 + self.core) * 4, 4)], self.own_sem
        )

    def start(self):
        for ch in range(4):
            src, dst = self.own.at[pl.ds(ch, 1)], self.rows(self.z, self.core, ch)
            for d in range(2):
                if self.has(d, 0, ch):
                    self.ring(src, dst, d, 0, ch).start()
        self.pair(self.own, self.rows(self.z, self.core, 0, 4), 0).start()
        self.own_copy().start()

    def step(self, k):
        z_from = [lax.rem(self.z - sign * (k + 1) + 2 * self.n, self.n) for sign in (1, -1)]
        for ch in range(4):
            for d in range(2):
                if not self.has(d, k, ch):
                    continue
                block = self.rows(z_from[d], self.core, ch)
                self.ring(block, block, d, k, ch).wait_recv()
                if self.has(d, k + 1, ch):
                    self.ring(block, block, d, k + 1, ch).start()
        for d in range(2):
            chunks = [ch for ch in range(4) if self.has(d, k, ch)]
            block = self.rows(z_from[d], self.core, chunks[0], len(chunks))
            self.pair(block, block, k + 1).start()

    def pair_wait(self, k):
        count = 4 if k == 0 else sum(self.has(d, k - 1, ch) for d in range(2) for ch in range(4))
        landed = self.out.at[pl.ds(0, count)]
        self.pair(landed, landed, k).wait_recv()

    def places(self, k):
        return [self.z] if k == 0 else [
            lax.rem(self.z + sign * k + self.n, self.n) for sign in ((1, -1) if k < self.steps else (1,))
        ]

    def drain(self):
        sent = self.out.at[pl.ds(0, (4 * self.n - 2) * 2)]
        self.pair(sent, sent, 0).wait_send()


def named_range(ids, segs, owner):
    start = owner * ADP_OWN

    def body(i, carry):
        low, high = carry
        v = ids[i]
        held = (v >= start) & (v < start + ADP_OWN)
        return (
            jnp.where(held, jnp.minimum(low, v), low),
            jnp.where(held, jnp.maximum(high, v), high),
        )

    return lax.fori_loop(0, segs, body, (start + ADP_OWN, start - 1))


def step_kernel(
    owners, tensors,
    ids, x_hbm, w_hbm, down_ref, up_ref, g_ref,
    po_ref, gi_ref, sums_ref,
    asum, xv, wv, acc, pk, ga, gk, gb, f1, f2, r1, r2, s1, s2, q1, q2, part, inbox, mine, total,
    in_sem, own_sem, gs_a, gr_a, gp_a, gs_b, gr_b, gp_b,
    s_r1, v_r1, s_r2, v_r2, s_q1, v_q1, s_q2, v_q2, ar_send, ar_recv,
):
    nz, nx = owners // 2, X_CHIPS
    ny = tensors // nx
    hx, hy = nx // 2, ny // 2
    me_a, me_t = lax.axis_index("adapter"), lax.axis_index("tensor")
    z, core = lax.div(me_a, 2), lax.rem(me_a, 2)
    y, x = lax.div(me_t, nx), lax.rem(me_t, nx)

    barrier = pltpu.get_barrier_semaphore()
    for to in (lax.rem(z + 1, nz) * 2 + core, lax.rem(z + nz - 1, nz) * 2 + core, z * 2 + 1 - core):
        pl.semaphore_signal(barrier, inc=1, device_id={"adapter": to}, device_id_type=MESH)

    def greet(d, carry):
        to = lax.rem(me_t + d, tensors)
        pl.semaphore_signal(barrier, inc=1, device_id={"tensor": to}, device_id_type=MESH)
        return carry

    lax.fori_loop(1, tensors, greet, 0)
    w_in = pltpu.make_async_copy(w_hbm, wv, in_sem.at[0])
    x_in = pltpu.make_async_copy(x_hbm, xv, in_sem.at[1])
    w_in.start()
    x_in.start()
    segs = owners * 2
    own_low, own_high = named_range(ids, segs, me_a)
    for j, v in enumerate((own_low, own_high)):
        local = jnp.clip(v - me_a * ADP_OWN, 0, ADP_OWN - 1)
        pk[j] = down_ref[local]
        pk[ACTIVE + j] = up_ref[local]

    panels = RingGather(nz, z, core, pk, ga, gs_a, gr_a, gp_a, own_sem.at[0])
    parts = RingGather(nz, z, core, gk, gb, gs_b, gr_b, gp_b, own_sem.at[1])
    along_x = lambda place: y * nx + place
    along_y = lambda place: place * nx + x
    sum_x1 = RingSum(nx, x, along_x, f1, r1, s_r1, v_r1)
    sum_y1 = RingSum(ny, y, along_y, f2, r2, s_r2, v_r2)
    sum_y2 = RingSum(ny, y, along_y, s1, q1, s_q1, v_q1)
    sum_x2 = RingSum(nx, x, along_x, s2, q2, s_q2, v_q2)

    pl.semaphore_wait(barrier, tensors + 2)
    panels.start()
    w_in.wait()

    def frozen_term(t, carry):
        term = dot(g_ref[...], wv[t], 1, 1).astype(BF16)
        ty, tx = lax.div(t, nx), lax.rem(t, nx)
        f1[tx, lax.div(ty, hy), lax.rem(ty, hy)] = term[:SEG_ROWS]
        f2[ty, lax.div(tx, hx), lax.rem(tx, hx)] = term[SEG_ROWS:]
        return carry

    lax.fori_loop(0, tensors // 2, frozen_term, 0)
    panels.step(0)
    lax.fori_loop(tensors // 2, tensors, frozen_term, 0)
    sum_x1.start()
    sum_y1.start()
    seg_block = []
    for s in range(2):
        v = ids[me_a * 2 + s]
        owner = lax.div(v, ADP_OWN)
        low, _ = named_range(ids, segs, owner)
        seg_block.append(owner * 4 + jnp.where(v > low, 1, 0))
    same = jnp.where(ids[me_a * 2] == ids[me_a * 2 + 1], 1.0, 0.0).astype(F32)
    asum[...] = jnp.zeros_like(asum)
    order = [(panels, 1), (panels, 2), (sum_y1, 0), (sum_x1, 0), (panels, 3), (panels, 4), (sum_y1, 1)]
    order += [(panels, k) for k in range(5, panels.steps)]
    for ring, k in order:
        if k < ring.steps:
            ring.step(k)
    panels.own_copy().wait()
    for k in range(panels.steps + 1):
        panels.pair_wait(k)

    x_in.wait()
    col0 = pl.multiple_of(me_t * COLS, COLS)
    for s in range(2):
        rows = slice(s * SEG_ROWS, (s + 1) * SEG_ROWS)
        low = dot(xv[rows, pl.ds(col0, COLS)], ga[seg_block[s]], 1, 1)
        back = dot(g_ref[rows, :], ga[seg_block[s] + ACTIVE], 1, 1)
        both = jnp.concatenate([low, back], axis=1)
        per = tensors // 2
        part[s * per:(s + 1) * per] = both.reshape(per, SEG_ROWS // per, 2 * RANK)

    def to_peer(src, dst, phase, d):
        return pltpu.make_async_remote_copy(
            src_ref=src, dst_ref=dst, send_sem=ar_send.at[phase], recv_sem=ar_recv.at[phase],
            device_id={"tensor": lax.rem(me_t + d, tensors)}, device_id_type=MESH,
        )

    def scatter(d, carry):
        to_peer(part.at[lax.rem(me_t + d, tensors)], inbox.at[d - 1], 0, d).start()
        return carry

    lax.fori_loop(1, tensors, scatter, 0)

    acc[...] = jnp.zeros_like(acc)

    def forward(k, carry):
        at = pl.multiple_of(k * COLS, COLS)
        acc[...] += dot(xv[:, pl.ds(at, COLS)], wv[k], 1, 0)
        return carry

    lax.fori_loop(0, tensors, forward, 0)

    others = inbox.at[pl.ds(0, tensors - 1)]
    to_peer(others, others, 0, 1).wait_recv()
    value = part[me_t]
    for d in range(tensors - 1):
        value = value + inbox[d]
    mine[...] = value
    total[me_t] = value

    def spread(d, carry):
        to_peer(mine, total.at[me_t], 1, d).start()
        return carry

    lax.fori_loop(1, tensors, spread, 0)

    for k in range(2, sum_y1.steps):
        sum_y1.step(k)
    sum_x1.finish()
    for h in range(2):
        def first_x(j, carry):
            v = sum_x1.total(h, j).astype(BF16)
            s1[h * hy + j, 0] = v[:RANK]
            s1[h * hy + j, 1] = v[RANK:]
            return carry

        lax.fori_loop(0, hy, first_x, 0)
    rest = total.at[pl.ds(0, tensors - 1)]
    to_peer(rest, rest, 1, 1).wait_recv()

    ranks = total[...].reshape(2 * SEG_ROWS, 2 * RANK)
    halves, downs, ups = [], [], []
    for s in range(2):
        rows = slice(s * SEG_ROWS, (s + 1) * SEG_ROWS)
        low_half = ranks[rows, :RANK].astype(BF16)
        back_half = (adapter_scale * ranks[rows, RANK:]).astype(BF16)
        halves.append((low_half, back_half))
        downs.append(dot(back_half, xv[rows, pl.ds(col0, COLS)], 0, 0))
        ups.append(adapter_scale * dot(low_half, g_ref[rows, :], 0, 0))
    for base, terms in ((0, downs), (ACTIVE, ups)):
        gk[base] = (terms[0] + same * terms[1]).astype(BF16)
        gk[base + 1] = ((1.0 - same) * terms[1]).astype(BF16)
    parts.start()
    sum_y2.start()
    for s in range(2):
        rows = slice(s * SEG_ROWS, (s + 1) * SEG_ROWS)
        low_half, back_half = halves[s]
        adapted = dot(low_half, ga[seg_block[s] + ACTIVE], 1, 0)
        po_ref[rows, :] = (acc[rows, :] + adapter_scale * adapted).astype(BF16)
        acc[rows, :] = dot(back_half, ga[seg_block[s]], 1, 0)

    def add_group(place, side):
        group = place * 2 + side
        for slot, v in enumerate((own_low, own_high)):
            hits = []
            for s in range(2):
                hit = ids[group * 2 + s] == v
                if slot:
                    hit = hit & (own_high != own_low)
                hits.append(jnp.where(hit, 1.0, 0.0).astype(F32))
            for du in range(2):
                at = group * 4 + du * 2
                asum[du * 2 + slot] += hits[0] * gb[at].astype(F32) + hits[1] * gb[at + 1].astype(F32)

    def add_side(k, side):
        for place in parts.places(k):
            add_group(place, side)

    def finish_y1():
        sum_y1.finish()
        for h in range(2):
            def first_y(j, carry):
                v = sum_y1.total(h, j).astype(BF16)
                s2[h * hx + j, 0] = v[:RANK]
                s2[h * hx + j, 1] = v[RANK:]
                return carry

            lax.fori_loop(0, hx, first_y, 0)
        sum_x2.start()

    def finish_frozen():
        sum_y2.finish()
        sum_x2.finish()
        for s, ring in ((0, sum_y2), (1, sum_x2)):
            for h in range(2):
                rows = slice(s * SEG_ROWS + h * RANK, s * SEG_ROWS + (h + 1) * RANK)
                gi_ref[rows, :] = (ring.total(h) + acc[rows, :]).astype(BF16)

    for k in range(max(parts.steps, sum_y2.steps)):
        if k < parts.steps:
            parts.step(k)
        if k == 0:
            finish_y1()
            parts.own_copy().wait()
            add_side(0, core)
        for ring, j in ((sum_y2, k), (sum_x2, k - 1)):
            if 0 <= j < ring.steps:
                ring.step(j)
        if k < parts.steps:
            parts.pair_wait(k)
            add_side(k, 1 - core)
            add_side(k + 1, core)
        if k == max(sum_y2.steps, sum_x2.steps + 1) - 1:
            finish_frozen()
    parts.pair_wait(parts.steps)
    add_side(parts.steps, 1 - core)
    sums_ref[...] = asum[...].astype(BF16)

    panels.drain()
    parts.drain()
    for ring in (sum_x1, sum_y1, sum_y2, sum_x2):
        ring.drain()
    to_peer(others, others, 0, 1).wait_send()
    to_peer(others, others, 1, 1).wait_send()


def place_kernel(segs, ids, po_in, gi_in, sums, po_ref, gi_ref, dg_ref, ug_ref):
    start = lax.axis_index("adapter") * ADP_OWN
    low, high = named_range(ids, segs, lax.axis_index("adapter"))
    po_ref[...] = po_in[...]
    gi_ref[...] = gi_in[...]
    for base, out in ((0, dg_ref), (ACTIVE, ug_ref)):
        def place(i, carry):
            first = jnp.where(start + i == low, 1.0, 0.0).astype(F32)
            second = jnp.where((start + i == high) & (high != low), 1.0, 0.0).astype(F32)
            out[i] = (first * sums[base].astype(F32) + second * sums[base + 1].astype(F32)).astype(BF16)
            return carry

        lax.fori_loop(0, ADP_OWN, place, 0)


def per_device(
    rollout_activations,
    projection_weight,
    adapter_down_panels,
    adapter_up_panels,
    output_gradient,
    segment_adapter,
):
    owners, tensors = lax.axis_size("adapter"), lax.axis_size("tensor")
    nz, nx = owners // 2, X_CHIPS
    ny = tensors // nx
    rows, width = rollout_activations.shape
    blocks = owners * 4
    slots_x, slots_y = chains_of(nx)[1], chains_of(ny)[1]
    vmem = pltpu.VMEM
    dma, block = pltpu.SemaphoreType.DMA, (RANK, COLS)
    gather_sems = [dma(()), dma((2, nz // 2, 4)), dma((nz // 2 + 1,))]
    seg = (SEG_ROWS, COLS)
    scratch = [
        vmem((4,) + block, F32),
        vmem((rows, width), BF16),
        vmem((tensors, COLS, COLS), BF16),
        vmem((rows, COLS), F32),
        vmem((4,) + block, BF16),
        vmem((blocks,) + block, BF16),
        vmem((4,) + block, BF16),
        vmem((blocks,) + block, BF16),
        vmem((nx, 2, ny // 2) + seg, BF16),
        vmem((ny, 2, nx // 2) + seg, BF16),
        vmem((slots_x, ny // 2) + seg, BF16),
        vmem((slots_y, nx // 2) + seg, BF16),
        vmem((ny, 2) + block, BF16),
        vmem((nx, 2) + block, BF16),
        vmem((slots_y,) + block, BF16),
        vmem((slots_x,) + block, BF16),
        vmem((tensors, rows // tensors, 2 * RANK), F32),
        vmem((tensors, rows // tensors, 2 * RANK), F32),
        vmem((rows // tensors, 2 * RANK), F32),
        vmem((tensors, rows // tensors, 2 * RANK), F32),
        dma((2,)),
        dma((2,)),
        *gather_sems,
        *gather_sems,
    ]
    for slots in (slots_x, slots_y, slots_y, slots_x):
        scratch += [dma(()), dma((slots,))]
    scratch += [dma((2,)), dma((2,))]
    smem, whole, any_space = (
        pl.BlockSpec(memory_space=pltpu.SMEM),
        pl.BlockSpec(memory_space=pltpu.VMEM),
        pl.BlockSpec(memory_space=pl.ANY),
    )
    like_rows = jax.ShapeDtypeStruct((rows, COLS), BF16)
    like_panels = jax.ShapeDtypeStruct((ADP_OWN,) + block, BF16)
    po, gi, sums = pl.pallas_call(
        functools.partial(step_kernel, owners, tensors),
        out_shape=[like_rows, like_rows, jax.ShapeDtypeStruct((4,) + block, BF16)],
        in_specs=[smem, any_space, any_space, whole, whole, whole],
        out_specs=[whole] * 3,
        scratch_shapes=scratch,
        compiler_params=pltpu.CompilerParams(
            collective_id=0, has_side_effects=True, vmem_limit_bytes=60 * 1024 * 1024
        ),
    )(
        segment_adapter,
        rollout_activations,
        projection_weight.reshape(tensors, COLS, COLS),
        adapter_down_panels,
        adapter_up_panels,
        output_gradient,
    )
    return tuple(
        pl.pallas_call(
            functools.partial(place_kernel, owners * 2),
            out_shape=[like_rows, like_rows, like_panels, like_panels],
            in_specs=[smem, whole, whole, whole],
            out_specs=[whole] * 4,
        )(segment_adapter, po, gi, sums)
    )


def solution(mesh):
    in_specs = (
        P("adapter", None),
        P(None, "tensor"),
        P("adapter", None, "tensor"),
        P("adapter", None, "tensor"),
        P("adapter", "tensor"),
        P(),
    )
    out_specs = (
        P("adapter", "tensor"),
        P("adapter", "tensor"),
        P("adapter", None, "tensor"),
        P("adapter", None, "tensor"),
    )
    return jax.shard_map(
        per_device, mesh=mesh, in_specs=in_specs, out_specs=out_specs, check_vma=False
    )
```

```python
import functools

import jax
import jax.numpy as jnp
from jax import lax
from jax.experimental import pallas as pl
from jax.experimental.pallas import tpu as pltpu
from jax.sharding import PartitionSpec as P

SEG_ROWS = 128
ADP_OWN = 16
ACTIVE = 2
RANK = 64
COLS = 256
X_CHIPS = 4
MESH = pl.DeviceIdType.MESH
F32 = jnp.float32
BF16 = jnp.bfloat16

adapter_scale = 0.5


def dot(a, b, ca, cb):
    return lax.dot_general(a, b, (((ca,), (cb,)), ((), ())), preferred_element_type=F32)


def chains_of(n):
    half = n // 2
    chains, base = [], 0
    for sign, part, length in ((1, 0, half), (-1, 1, half), (1, 1, half - 1), (-1, 0, half - 1)):
        if length:
            chains.append((sign, part, length, base))
            base += length
    return chains, base


class RingSum:
    def __init__(self, n, pos, device_of, src, land, send_sem, recv_sem):
        self.n, self.pos, self.device_of = n, pos, device_of
        self.src, self.land, self.send_sem, self.recv_sem = src, land, send_sem, recv_sem
        self.chains, _ = chains_of(n)
        self.steps = n // 2

    def at(self, offset):
        return lax.rem(self.pos + offset + self.n, self.n)

    def copy(self, src, slot, sign):
        return pltpu.make_async_remote_copy(
            src_ref=src,
            dst_ref=self.land.at[slot],
            send_sem=self.send_sem,
            recv_sem=self.recv_sem.at[slot],
            device_id={"tensor": self.device_of(self.at(sign))},
            device_id_type=MESH,
        )

    def start(self):
        for sign, part, length, base in self.chains:
            self.copy(self.src.at[self.at(sign * length), part], base, sign).start()

    def step(self, s):
        for sign, part, length, base in self.chains:
            if s >= length - 1:
                continue
            slot = base + s
            self.copy(self.land.at[slot], slot, sign).wait_recv()
            place = self.at(sign * (length - s - 1))
            self.add(slot, place, part)
            self.copy(self.land.at[slot], slot + 1, sign).start()

    def add(self, slot, place, part):
        if len(self.land.shape) == 3:
            total = self.land[slot].astype(F32) + self.src[place, part].astype(F32)
            self.land[slot] = total.astype(BF16)
            return

        def body(j, carry):
            total = self.land[slot, j].astype(F32) + self.src[place, part, j].astype(F32)
            self.land[slot, j] = total.astype(BF16)
            return carry

        lax.fori_loop(0, self.land.shape[1], body, 0)

    def finish(self):
        for sign, part, length, base in self.chains:
            slot = base + length - 1
            self.copy(self.land.at[slot], slot, sign).wait_recv()

    def lasts(self, part):
        return [base + length - 1 for _, p, length, base in self.chains if p == part]

    def total(self, part, *index):
        value = self.src[(self.pos, part) + index].astype(F32)
        for slot in self.lasts(part):
            value = value + self.land[(slot,) + index].astype(F32)
        return value

    def drain(self):
        whole = self.src.at[pl.ds(0, self.n - 1)]
        pltpu.make_async_remote_copy(
            src_ref=whole,
            dst_ref=whole,
            send_sem=self.send_sem,
            recv_sem=self.recv_sem.at[0],
            device_id={"tensor": self.device_of(self.at(1))},
            device_id_type=MESH,
        ).wait_send()


class RingGather:
    def __init__(self, n, z, core, own, out, send_sem, recv_sem, pair_sem, own_sem):
        self.n, self.z, self.core = n, z, core
        self.own, self.out = own, out
        self.send_sem, self.recv_sem, self.pair_sem, self.own_sem = send_sem, recv_sem, pair_sem, own_sem
        self.steps = n // 2

    def has(self, d, k, ch):
        return k < self.steps - 1 or (k == self.steps - 1 and d == ch // 2)

    def rows(self, z, core, ch, count=1):
        return self.out.at[pl.ds((z * 2 + core) * 4 + ch, count)]

    def ring(self, src, dst, d, k, ch):
        sign = 1 - 2 * d
        z_to = lax.rem(self.z + sign + self.n, self.n)
        return pltpu.make_async_remote_copy(
            src_ref=src,
            dst_ref=dst,
            send_sem=self.send_sem,
            recv_sem=self.recv_sem.at[d, k, ch],
            device_id={"adapter": z_to * 2 + self.core},
            device_id_type=MESH,
        )

    def pair(self, src, dst, k):
        return pltpu.make_async_remote_copy(
            src_ref=src,
            dst_ref=dst,
            send_sem=self.send_sem,
            recv_sem=self.pair_sem.at[k],
            device_id={"adapter": self.z * 2 + 1 - self.core},
            device_id_type=MESH,
        )

    def own_copy(self):
        return pltpu.make_async_copy(
            self.own, self.out.at[pl.ds((self.z * 2 + self.core) * 4, 4)], self.own_sem
        )

    def start(self):
        for ch in range(4):
            src, dst = self.own.at[pl.ds(ch, 1)], self.rows(self.z, self.core, ch)
            for d in range(2):
                if self.has(d, 0, ch):
                    self.ring(src, dst, d, 0, ch).start()
        self.pair(self.own, self.rows(self.z, self.core, 0, 4), 0).start()
        self.own_copy().start()

    def step(self, k):
        z_from = [lax.rem(self.z - sign * (k + 1) + 2 * self.n, self.n) for sign in (1, -1)]
        for ch in range(4):
            for d in range(2):
                if not self.has(d, k, ch):
                    continue
                block = self.rows(z_from[d], self.core, ch)
                self.ring(block, block, d, k, ch).wait_recv()
                if self.has(d, k + 1, ch):
                    self.ring(block, block, d, k + 1, ch).start()
        for d in range(2):
            chunks = [ch for ch in range(4) if self.has(d, k, ch)]
            block = self.rows(z_from[d], self.core, chunks[0], len(chunks))
            self.pair(block, block, k + 1).start()

    def pair_wait(self, k):
        count = 4 if k == 0 else sum(self.has(d, k - 1, ch) for d in range(2) for ch in range(4))
        landed = self.out.at[pl.ds(0, count)]
        self.pair(landed, landed, k).wait_recv()

    def places(self, k):
        return [self.z] if k == 0 else [
            lax.rem(self.z + sign * k + self.n, self.n) for sign in ((1, -1) if k < self.steps else (1,))
        ]

    def drain(self):
        sent = self.out.at[pl.ds(0, (4 * self.n - 2) * 2)]
        self.pair(sent, sent, 0).wait_send()


def named_range(ids, segs, owner):
    start = owner * ADP_OWN

    def body(i, carry):
        low, high = carry
        v = ids[i]
        held = (v >= start) & (v < start + ADP_OWN)
        return (
            jnp.where(held, jnp.minimum(low, v), low),
            jnp.where(held, jnp.maximum(high, v), high),
        )

    return lax.fori_loop(0, segs, body, (start + ADP_OWN, start - 1))


def step_kernel(
    owners, tensors,
    ids, x_hbm, w_hbm, down_ref, up_ref, g_ref,
    po_ref, gi_ref, sums_ref,
    asum, xv, wv, acc, pk, ga, gk, gb, f1, f2, r1, r2, s1, s2, q1, q2, part, inbox, mine, total,
    in_sem, own_sem, gs_a, gr_a, gp_a, gs_b, gr_b, gp_b,
    s_r1, v_r1, s_r2, v_r2, s_q1, v_q1, s_q2, v_q2, ar_send, ar_recv, told,
):
    nz, nx = owners // 2, X_CHIPS
    ny = tensors // nx
    hx, hy = nx // 2, ny // 2
    me_a, me_t = lax.axis_index("adapter"), lax.axis_index("tensor")
    z, core = lax.div(me_a, 2), lax.rem(me_a, 2)
    y, x = lax.div(me_t, nx), lax.rem(me_t, nx)

    barrier = pltpu.get_barrier_semaphore()
    for to in (lax.rem(z + 1, nz) * 2 + core, lax.rem(z + nz - 1, nz) * 2 + core, z * 2 + 1 - core):
        pl.semaphore_signal(barrier, inc=1, device_id={"adapter": to}, device_id_type=MESH)
    x_sides = [y * nx + lax.rem(x + 1, nx), y * nx + lax.rem(x + nx - 1, nx)]
    y_sides = [lax.rem(y + 1, ny) * nx + x, lax.rem(y + ny - 1, ny) * nx + x]
    for to in x_sides + y_sides:
        pl.semaphore_signal(barrier, inc=1, device_id={"tensor": to}, device_id_type=MESH)
    rounds = [y_sides] * (ny // 2 - 1) + [x_sides] * (nx // 2)

    def tell(k):
        if k < len(rounds):
            for to in rounds[k]:
                pl.semaphore_signal(told.at[k], inc=1, device_id={"tensor": to}, device_id_type=MESH)

    def hear(k):
        if k < len(rounds):
            pl.semaphore_wait(told.at[k], 2)
            tell(k + 1)

    w_in = pltpu.make_async_copy(w_hbm, wv, in_sem.at[0])
    x_in = pltpu.make_async_copy(x_hbm, xv, in_sem.at[1])
    w_in.start()
    x_in.start()
    segs = owners * 2
    own_low, own_high = named_range(ids, segs, me_a)
    for j, v in enumerate((own_low, own_high)):
        local = jnp.clip(v - me_a * ADP_OWN, 0, ADP_OWN - 1)
        pk[j] = down_ref[local]
        pk[ACTIVE + j] = up_ref[local]

    panels = RingGather(nz, z, core, pk, ga, gs_a, gr_a, gp_a, own_sem.at[0])
    parts = RingGather(nz, z, core, gk, gb, gs_b, gr_b, gp_b, own_sem.at[1])
    along_x = lambda place: y * nx + place
    along_y = lambda place: place * nx + x
    sum_x1 = RingSum(nx, x, along_x, f1, r1, s_r1, v_r1)
    sum_y1 = RingSum(ny, y, along_y, f2, r2, s_r2, v_r2)
    sum_y2 = RingSum(ny, y, along_y, s1, q1, s_q1, v_q1)
    sum_x2 = RingSum(nx, x, along_x, s2, q2, s_q2, v_q2)

    pl.semaphore_wait(barrier, 7)
    panels.start()
    tell(0)
    w_in.wait()

    def frozen_term(t, carry):
        term = dot(g_ref[...], wv[t], 1, 1).astype(BF16)
        ty, tx = lax.div(t, nx), lax.rem(t, nx)
        f1[tx, lax.div(ty, hy), lax.rem(ty, hy)] = term[:SEG_ROWS]
        f2[ty, lax.div(tx, hx), lax.rem(tx, hx)] = term[SEG_ROWS:]
        return carry

    lax.fori_loop(0, tensors // 2, frozen_term, 0)
    panels.step(0)
    hear(0)
    lax.fori_loop(tensors // 2, tensors, frozen_term, 0)
    sum_x1.start()
    sum_y1.start()
    seg_block = []
    for s in range(2):
        v = ids[me_a * 2 + s]
        owner = lax.div(v, ADP_OWN)
        low, _ = named_range(ids, segs, owner)
        seg_block.append(owner * 4 + jnp.where(v > low, 1, 0))
    same = jnp.where(ids[me_a * 2] == ids[me_a * 2 + 1], 1.0, 0.0).astype(F32)
    asum[...] = jnp.zeros_like(asum)
    order = [(panels, 1), (panels, 2), (sum_y1, 0), (sum_x1, 0), (panels, 3), (panels, 4), (sum_y1, 1)]
    order += [(panels, k) for k in range(5, panels.steps)]
    for ring, k in order:
        if k < ring.steps:
            ring.step(k)
        if ring is panels:
            hear(k)
    for k in range(panels.steps, len(rounds)):
        hear(k)
    panels.own_copy().wait()
    for k in range(panels.steps + 1):
        panels.pair_wait(k)

    x_in.wait()
    col0 = pl.multiple_of(me_t * COLS, COLS)
    for s in range(2):
        rows = slice(s * SEG_ROWS, (s + 1) * SEG_ROWS)
        low = dot(xv[rows, pl.ds(col0, COLS)], ga[seg_block[s]], 1, 1)
        back = dot(g_ref[rows, :], ga[seg_block[s] + ACTIVE], 1, 1)
        both = jnp.concatenate([low, back], axis=1)
        per = tensors // 2
        part[s * per:(s + 1) * per] = both.reshape(per, SEG_ROWS // per, 2 * RANK)

    peers = [(dy, dx) for dy in range(ny) for dx in range(nx) if dy or dx]
    peers.sort(key=lambda p: (-min(p[0], ny - p[0]) - min(p[1], nx - p[1]), p))

    def place_of(peer):
        return lax.rem(y + peer[0], ny) * nx + lax.rem(x + peer[1], nx)

    def to_peer(src, dst, phase, peer):
        return pltpu.make_async_remote_copy(
            src_ref=src, dst_ref=dst, send_sem=ar_send.at[phase], recv_sem=ar_recv.at[phase],
            device_id={"tensor": place_of(peer)}, device_id_type=MESH,
        )

    for i, peer in enumerate(peers):
        to_peer(part.at[place_of(peer)], inbox.at[i], 0, peer).start()

    acc[...] = jnp.zeros_like(acc)

    def forward(k, carry):
        at = pl.multiple_of(k * COLS, COLS)
        acc[...] += dot(xv[:, pl.ds(at, COLS)], wv[k], 1, 0)
        return carry

    lax.fori_loop(0, tensors, forward, 0)

    others = inbox.at[pl.ds(0, tensors - 1)]
    to_peer(others, others, 0, peers[-1]).wait_recv()
    value = part[me_t]
    for d in range(tensors - 1):
        value = value + inbox[d]
    mine[...] = value
    total[me_t] = value

    for peer in peers:
        to_peer(mine, total.at[me_t], 1, peer).start()

    for k in range(2, sum_y1.steps):
        sum_y1.step(k)
    sum_x1.finish()
    for h in range(2):
        def first_x(j, carry):
            v = sum_x1.total(h, j).astype(BF16)
            s1[h * hy + j, 0] = v[:RANK]
            s1[h * hy + j, 1] = v[RANK:]
            return carry

        lax.fori_loop(0, hy, first_x, 0)
    rest = total.at[pl.ds(0, tensors - 1)]
    to_peer(rest, rest, 1, peers[-1]).wait_recv()

    ranks = total[...].reshape(2 * SEG_ROWS, 2 * RANK)
    halves, downs, ups = [], [], []
    for s in range(2):
        rows = slice(s * SEG_ROWS, (s + 1) * SEG_ROWS)
        low_half = ranks[rows, :RANK].astype(BF16)
        back_half = (adapter_scale * ranks[rows, RANK:]).astype(BF16)
        halves.append((low_half, back_half))
        downs.append(dot(back_half, xv[rows, pl.ds(col0, COLS)], 0, 0))
        ups.append(adapter_scale * dot(low_half, g_ref[rows, :], 0, 0))
    for base, terms in ((0, downs), (ACTIVE, ups)):
        gk[base] = (terms[0] + same * terms[1]).astype(BF16)
        gk[base + 1] = ((1.0 - same) * terms[1]).astype(BF16)
    parts.start()
    sum_y2.start()
    for s in range(2):
        rows = slice(s * SEG_ROWS, (s + 1) * SEG_ROWS)
        low_half, back_half = halves[s]
        adapted = dot(low_half, ga[seg_block[s] + ACTIVE], 1, 0)
        po_ref[rows, :] = (acc[rows, :] + adapter_scale * adapted).astype(BF16)
        acc[rows, :] = dot(back_half, ga[seg_block[s]], 1, 0)

    def add_group(place, side):
        group = place * 2 + side
        for slot, v in enumerate((own_low, own_high)):
            hits = []
            for s in range(2):
                hit = ids[group * 2 + s] == v
                if slot:
                    hit = hit & (own_high != own_low)
                hits.append(jnp.where(hit, 1.0, 0.0).astype(F32))
            for du in range(2):
                at = group * 4 + du * 2
                asum[du * 2 + slot] += hits[0] * gb[at].astype(F32) + hits[1] * gb[at + 1].astype(F32)

    def add_side(k, side):
        for place in parts.places(k):
            add_group(place, side)

    def finish_y1():
        sum_y1.finish()
        for h in range(2):
            def first_y(j, carry):
                v = sum_y1.total(h, j).astype(BF16)
                s2[h * hx + j, 0] = v[:RANK]
                s2[h * hx + j, 1] = v[RANK:]
                return carry

            lax.fori_loop(0, hx, first_y, 0)
        sum_x2.start()

    def finish_frozen():
        sum_y2.finish()
        sum_x2.finish()
        for s, ring in ((0, sum_y2), (1, sum_x2)):
            for h in range(2):
                rows = slice(s * SEG_ROWS + h * RANK, s * SEG_ROWS + (h + 1) * RANK)
                gi_ref[rows, :] = (ring.total(h) + acc[rows, :]).astype(BF16)

    for k in range(max(parts.steps, sum_y2.steps)):
        if k < parts.steps:
            parts.step(k)
        if k == 0:
            finish_y1()
            parts.own_copy().wait()
            add_side(0, core)
        for ring, j in ((sum_y2, k), (sum_x2, k - 1)):
            if 0 <= j < ring.steps:
                ring.step(j)
        if k < parts.steps:
            parts.pair_wait(k)
            add_side(k, 1 - core)
            add_side(k + 1, core)
        if k == max(sum_y2.steps, sum_x2.steps + 1) - 1:
            finish_frozen()
    parts.pair_wait(parts.steps)
    add_side(parts.steps, 1 - core)
    sums_ref[...] = asum[...].astype(BF16)

    panels.drain()
    parts.drain()
    for ring in (sum_x1, sum_y1, sum_y2, sum_x2):
        ring.drain()
    to_peer(others, others, 0, peers[-1]).wait_send()
    to_peer(others, others, 1, peers[-1]).wait_send()


def place_kernel(segs, ids, po_in, gi_in, sums, po_ref, gi_ref, dg_ref, ug_ref):
    start = lax.axis_index("adapter") * ADP_OWN
    low, high = named_range(ids, segs, lax.axis_index("adapter"))
    po_ref[...] = po_in[...]
    gi_ref[...] = gi_in[...]
    for base, out in ((0, dg_ref), (ACTIVE, ug_ref)):
        def place(i, carry):
            other = jnp.where(start + i == high, sums[base + 1], jnp.zeros((RANK, COLS), BF16))
            out[i] = jnp.where(start + i == low, sums[base], other)
            return carry

        lax.fori_loop(0, ADP_OWN, place, 0)


def per_device(
    rollout_activations,
    projection_weight,
    adapter_down_panels,
    adapter_up_panels,
    output_gradient,
    segment_adapter,
):
    owners, tensors = lax.axis_size("adapter"), lax.axis_size("tensor")
    nz, nx = owners // 2, X_CHIPS
    ny = tensors // nx
    rows, width = rollout_activations.shape
    blocks = owners * 4
    slots_x, slots_y = chains_of(nx)[1], chains_of(ny)[1]
    vmem = pltpu.VMEM
    dma, block = pltpu.SemaphoreType.DMA, (RANK, COLS)
    gather_sems = [dma(()), dma((2, nz // 2, 4)), dma((nz // 2 + 1,))]
    seg = (SEG_ROWS, COLS)
    scratch = [
        vmem((4,) + block, F32),
        vmem((rows, width), BF16),
        vmem((tensors, COLS, COLS), BF16),
        vmem((rows, COLS), F32),
        vmem((4,) + block, BF16),
        vmem((blocks,) + block, BF16),
        vmem((4,) + block, BF16),
        vmem((blocks,) + block, BF16),
        vmem((nx, 2, ny // 2) + seg, BF16),
        vmem((ny, 2, nx // 2) + seg, BF16),
        vmem((slots_x, ny // 2) + seg, BF16),
        vmem((slots_y, nx // 2) + seg, BF16),
        vmem((ny, 2) + block, BF16),
        vmem((nx, 2) + block, BF16),
        vmem((slots_y,) + block, BF16),
        vmem((slots_x,) + block, BF16),
        vmem((tensors, rows // tensors, 2 * RANK), F32),
        vmem((tensors, rows // tensors, 2 * RANK), F32),
        vmem((rows // tensors, 2 * RANK), F32),
        vmem((tensors, rows // tensors, 2 * RANK), F32),
        dma((2,)),
        dma((2,)),
        *gather_sems,
        *gather_sems,
    ]
    for slots in (slots_x, slots_y, slots_y, slots_x):
        scratch += [dma(()), dma((slots,))]
    scratch += [dma((2,)), dma((2,)), pltpu.SemaphoreType.REGULAR((ny // 2 - 1 + nx // 2,))]
    smem, whole, any_space = (
        pl.BlockSpec(memory_space=pltpu.SMEM),
        pl.BlockSpec(memory_space=pltpu.VMEM),
        pl.BlockSpec(memory_space=pl.ANY),
    )
    like_rows = jax.ShapeDtypeStruct((rows, COLS), BF16)
    like_panels = jax.ShapeDtypeStruct((ADP_OWN,) + block, BF16)
    po, gi, sums = pl.pallas_call(
        functools.partial(step_kernel, owners, tensors),
        out_shape=[like_rows, like_rows, jax.ShapeDtypeStruct((4,) + block, BF16)],
        in_specs=[smem, any_space, any_space, whole, whole, whole],
        out_specs=[whole] * 3,
        scratch_shapes=scratch,
        compiler_params=pltpu.CompilerParams(
            collective_id=0, has_side_effects=True, vmem_limit_bytes=60 * 1024 * 1024
        ),
    )(
        segment_adapter,
        rollout_activations,
        projection_weight.reshape(tensors, COLS, COLS),
        adapter_down_panels,
        adapter_up_panels,
        output_gradient,
    )
    return tuple(
        pl.pallas_call(
            functools.partial(place_kernel, owners * 2),
            out_shape=[like_rows, like_rows, like_panels, like_panels],
            in_specs=[smem, whole, whole, whole],
            out_specs=[whole] * 4,
        )(segment_adapter, po, gi, sums)
    )


def solution(mesh):
    in_specs = (
        P("adapter", None),
        P(None, "tensor"),
        P("adapter", None, "tensor"),
        P("adapter", None, "tensor"),
        P("adapter", "tensor"),
        P(),
    )
    out_specs = (
        P("adapter", "tensor"),
        P("adapter", "tensor"),
        P("adapter", None, "tensor"),
        P("adapter", None, "tensor"),
    )
    return jax.shard_map(
        per_device, mesh=mesh, in_specs=in_specs, out_specs=out_specs, check_vma=False
    )
```
